256 devices in a mesh: fsdp: 64 (over y, z, core), tensor: 4 (over x).
Axes of the slice: x: 4, y: 4, z: 8, core: 2. Of those that a mesh axis runs over, the one named last changes fastest.
Arguments:
- layer_input: bfloat16 [16384, 8192], P('fsdp', 'tensor'), may hold values from -6 to 6
- value_grad: bfloat16 [16384, 1024], P('fsdp', 'tensor'), may hold values from -6 to 6
- quant_codes: int32 [8192, 1024], P('fsdp', 'tensor'), may hold values from 0 to 15
- block_scales: float32 [8192, 16], P('fsdp', 'tensor'), may hold values from 0.02 to 0.08
- tenant_ids: int32 [1024], P('fsdp'), may hold values from 0 to 63
- live_counts: int32 [64], P('fsdp'), may hold values from 12 to 16, as said below
- tenant_owner: int32 [64], replicated, may hold values from 0 to 63, each once
- factor_down: float32 [64, 16, 8192], P('fsdp', None, 'tensor'), may hold values from -6 to 6
- factor_up: float32 [64, 16, 1024], P('fsdp', None, 'tensor'), may hold values from -6 to 6
- moment_down: float32 [64, 16, 8192], P('fsdp', None, 'tensor'), may hold values from -6 to 6
- second_down: float32 [64, 16, 8192], P('fsdp', None, 'tensor'), may hold values from 0.05 to 5
- moment_up: float32 [64, 16, 1024], P('fsdp', None, 'tensor'), may hold values from -6 to 6
- second_up: float32 [64, 16, 1024], P('fsdp', None, 'tensor'), may hold values from 0.05 to 5
Outputs:
- layer_input_gradient: bfloat16 [16384, 8192], P('fsdp', 'tensor')
- new_down: float32 [64, 16, 8192], P('fsdp', None, 'tensor')
- new_up: float32 [64, 16, 1024], P('fsdp', None, 'tensor')
- new_moment_down: float32 [64, 16, 8192], P('fsdp', None, 'tensor')
- new_second_down: float32 [64, 16, 8192], P('fsdp', None, 'tensor')
- new_moment_up: float32 [64, 16, 1024], P('fsdp', None, 'tensor')
- new_second_up: float32 [64, 16, 1024], P('fsdp', None, 'tensor')
The draws below stay inside these ranges and needn't reach their ends.
Inputs may be any that keep to these rules, and one draw needn't show every extreme that they name: The first live_counts[f] sequence slots of fsdp index f are live and the rest are padding; some index has all 16 live. tenant_owner is a permutation: tenant t's adapter and its moments sit in slot tenant_owner[t].
All inputs are finite; a program needn't handle non-finite values.
Results may differ from the reference program's by a relative error of at most 0.01.
Values may be sent and summed in bfloat16 or wider, within the bound.
No kernel may reach another device: no remote copies, remote signals or barrier semaphores. Data moves between devices by JAX's collectives and lax.ppermute only.
A program may use at most 128 MiB of HBM per device.

```python
import math
import jax
import jax.numpy as jnp
from jax import lax

MODEL_WIDTH = 8192
ADAPTER_RANK = 16
QB = 64
SEQ = 16
SLOTS = 16
KV = 1024
TENANTS = 64
TOKEN_TOTAL = 16384
N_FSDP = 64


def draw_live_counts(key, part):
    counts = jax.random.randint(key, (N_FSDP,), SLOTS * 3 // 4, SLOTS + 1, dtype=jnp.int32)
    chosen = jax.random.randint(jax.random.fold_in(key, 7), (), 0, N_FSDP, dtype=jnp.int32)
    filled = jnp.where(jnp.arange(N_FSDP, dtype=jnp.int32) == chosen, SLOTS, counts)
    return filled.astype(jnp.int32)


def place_ends(entries, rng, low, high):
    dims = entries.shape
    spot = [jax.random.randint(jax.random.fold_in(rng, axis), (), 0, dims[axis]) for axis in range(len(dims))]
    entries = entries.at[tuple(spot)].set(low)
    longest = dims.index(max(dims))
    spot[longest] = (spot[longest] + 1) % dims[longest]
    return entries.at[tuple(spot)].set(high)


def block_levels(own_key, extent, pieces, smallest, high):
    factor_of, own = 1.0, jax.random.fold_in(own_key, 6)
    for dim, blocks in pieces:
        heights = jnp.exp(jax.random.uniform(jax.random.fold_in(own, dim), (blocks,), jnp.float32, smallest / len(pieces), high / len(pieces)))
        factor_of = factor_of * jnp.repeat(heights, extent[dim] // blocks).reshape([-1 if axis == dim else 1 for axis in range(len(extent))])
    return factor_of


def noise(rng, shape, scale, bound, cuts=(), kind=jnp.bfloat16):
    entries = jax.random.normal(rng, shape, jnp.float32) * scale
    if len(cuts) > 0:
        entries = block_levels(rng, shape, cuts, -0.22, 0.18) * entries
    return jnp.clip(entries, min=-bound, max=bound).astype(kind)


def setup_inputs(seed: int = 0) -> dict:
    keys = jax.random.split(jax.random.key(seed), 14)
    layer_input = noise(keys[0], (TOKEN_TOTAL, MODEL_WIDTH), 1.0, 6.0, ((0, 64), (1, 4)))
    value_grad = noise(keys[1], (TOKEN_TOTAL, KV), 1.0, 6.0, ((0, 64), (1, 4)))
    quant_codes = place_ends(jax.random.randint(keys[2], (MODEL_WIDTH, KV), 0, 16), jax.random.fold_in(keys[2], 1), 0, 15).astype(jnp.int32)
    block_scales = jnp.clip(jnp.exp(math.log(0.08) - 1.3862944 * jax.random.uniform(keys[3], (MODEL_WIDTH, KV // QB), jnp.float32) ** block_levels(keys[3], (MODEL_WIDTH, KV // QB), ((0, 64), (1, 4)), -0.2, 0.2)), 0.02, 0.08)
    tenant_ids = place_ends(jax.random.randint(keys[4], (N_FSDP * SLOTS,), 0, TENANTS), jax.random.fold_in(keys[4], 1), 0, TENANTS - 1).astype(jnp.int32)
    live_counts = draw_live_counts(jax.random.fold_in(keys[13], 71), 0)
    tenant_owner = jax.random.permutation(keys[6], TENANTS).astype(jnp.int32)
    factor_down = noise(keys[7], (TENANTS, ADAPTER_RANK, MODEL_WIDTH), 1.0, 6.0, ((0, 64), (2, 4)), jnp.float32)
    factor_up = noise(keys[8], (TENANTS, ADAPTER_RANK, KV), 1.0, 6.0, ((0, 64), (2, 4)), jnp.float32)
    moment_down = noise(keys[9], (TENANTS, ADAPTER_RANK, MODEL_WIDTH), 1.0, 6.0, ((0, 64), (2, 4)), jnp.float32)
    second_down = jnp.clip(jnp.exp(math.log(5.0) - 4.6051702 * jax.random.uniform(keys[10], (TENANTS, ADAPTER_RANK, MODEL_WIDTH), jnp.float32) ** block_levels(keys[10], (TENANTS, ADAPTER_RANK, MODEL_WIDTH), ((0, 64), (2, 4)), -0.2, 0.2)), 0.05, 5.0)
    moment_up = noise(keys[11], (TENANTS, ADAPTER_RANK, KV), 1.0, 6.0, ((0, 64), (2, 4)), jnp.float32)
    second_up = jnp.clip(jnp.exp(math.log(5.0) - 4.6051702 * jax.random.uniform(keys[12], (TENANTS, ADAPTER_RANK, KV), jnp.float32) ** block_levels(keys[12], (TENANTS, ADAPTER_RANK, KV), ((0, 64), (2, 4)), -0.2, 0.2)), 0.05, 5.0)
    return dict(layer_input=layer_input, value_grad=value_grad, quant_codes=quant_codes, block_scales=block_scales, tenant_ids=tenant_ids, live_counts=live_counts, tenant_owner=tenant_owner, factor_down=factor_down, factor_up=factor_up, moment_down=moment_down, second_down=second_down, moment_up=moment_up, second_up=second_up)


nf4_levels = (-1.0, -0.6962, -0.5251, -0.3949, -0.2844, -0.1848, -0.0911, 0.0, 0.0796, 0.1609, 0.2461, 0.3379, 0.4407, 0.5626, 0.723, 1.0)
adapter_scale = 2.0
beta_one = 0.9
beta_two = 0.999
adam_step = 10.0
learn_rate = 0.05
decay_rate = 0.01
adam_eps = 1e-08

def adam_update(param, grad, moment, second):
    new_moment = beta_one * moment + (1.0 - beta_one) * grad
    new_second = beta_two * second + (1.0 - beta_two) * grad * grad
    corrected = new_moment / (1.0 - beta_one ** adam_step)
    divisor = jnp.sqrt(new_second / (1.0 - beta_two ** adam_step)) + adam_eps
    new_param = param - learn_rate * (corrected / divisor + decay_rate * param)
    return (new_param, new_moment, new_second)

def rounded_lower(values):
    lowered = lax.optimization_barrier(values.astype(jnp.bfloat16))
    return lowered.astype(jnp.float32)

def reference(layer_input, value_grad, quant_codes, block_scales, tenant_ids, live_counts, tenant_owner, factor_down, factor_up, moment_down, second_down, moment_up, second_up):
    table = jnp.array(nf4_levels, jnp.float32)
    weight = (jnp.take(table, quant_codes, axis=0) * jnp.repeat(block_scales, QB, axis=1)).astype(jnp.bfloat16)
    seq_index = jnp.arange(N_FSDP * SLOTS, dtype=jnp.int32)
    live_seq = seq_index % SLOTS < jnp.take(live_counts, seq_index // SLOTS, axis=0)
    live_tok = jnp.repeat(live_seq, SEQ)
    masked = jnp.where(live_tok[:, None], value_grad, jnp.zeros_like(value_grad))
    owner_seq = jnp.take(tenant_owner, tenant_ids, axis=0).astype(jnp.int32)
    down_low = factor_down.astype(jnp.bfloat16)
    up_low = factor_up.astype(jnp.bfloat16)
    inverse_width = 1.0 / math.sqrt(MODEL_WIDTH)
    coefficient = adapter_scale / math.sqrt(ADAPTER_RANK)
    base_weight = jnp.dot(masked, weight.T, preferred_element_type=jnp.float32)
    upper_level = lax.Precision.HIGHEST
    block_inputs = layer_input.reshape(N_FSDP, SLOTS, SEQ, MODEL_WIDTH)
    block_gradients = masked.reshape(N_FSDP, SLOTS, SEQ, KV)
    block_owners = owner_seq.reshape(N_FSDP, SLOTS)
    tenant_iota = jnp.arange(TENANTS, dtype=jnp.int32)

    def block_stride(carry, block):
        accumulated_down, accumulated_up = carry
        block_input, block_grad, block_owner = block
        sequence_down = jnp.take(down_low, block_owner, axis=0).astype(jnp.float32)
        sequence_up = jnp.take(up_low, block_owner, axis=0).astype(jnp.float32)
        widened_input = block_input.astype(jnp.float32)
        widened_gradient = block_grad.astype(jnp.float32)
        adapter_input = jnp.einsum('aol,ail->aoi', widened_input, sequence_down, precision=upper_level) * inverse_width
        adapter_gradient = jnp.einsum('qbt,qxt->qbx', widened_gradient, sequence_up, precision=upper_level) * coefficient
        input_lowrank = rounded_lower(adapter_input)
        gradient_lowrank = rounded_lower(adapter_gradient)
        adapter_input_gradient = jnp.einsum('pym,pme->pye', gradient_lowrank, sequence_down, precision=upper_level) * inverse_width
        part_down = jnp.einsum('nsr,nsd->nrd', gradient_lowrank, widened_input, precision=upper_level) * inverse_width
        part_up = jnp.einsum('nsr,nsc->nrc', input_lowrank, widened_gradient, precision=upper_level) * coefficient
        onehot = (block_owner[:, None] == tenant_iota[None, :]).astype(jnp.float32)
        accumulated_down = accumulated_down + jnp.einsum('nt,nrd->trd', onehot, part_down, precision=upper_level)
        accumulated_up = accumulated_up + jnp.einsum('nt,nrc->trc', onehot, part_up, precision=upper_level)
        return ((accumulated_down, accumulated_up), adapter_input_gradient)
    start_offset = (jnp.zeros((TENANTS, ADAPTER_RANK, MODEL_WIDTH), jnp.float32), jnp.zeros((TENANTS, ADAPTER_RANK, KV), jnp.float32))
    (down_gradient, up_gradient), adapter_parts = lax.scan(block_stride, start_offset, (block_inputs, block_gradients, block_owners))
    layer_input_gradient = (base_weight + adapter_parts.reshape(TOKEN_TOTAL, MODEL_WIDTH)).astype(jnp.bfloat16)
    new_down, new_moment_down, new_second_down = adam_update(factor_down, down_gradient, moment_down, second_down)
    new_up, new_moment_up, new_second_up = adam_update(factor_up, up_gradient, moment_up, second_up)
    return (layer_input_gradient, new_down, new_up, new_moment_down, new_second_down, new_moment_up, new_second_up)
```

```python
import math

import jax
import jax.numpy as jnp
from jax import lax
from jax.experimental import pallas as pl
from jax.experimental.pallas import tpu as pltpu
from jax.sharding import PartitionSpec as P

MODEL_WIDTH = 8192
ADAPTER_RANK = 16
NY, NZ, NC, NX = 4, 8, 2, 4


nf4_levels = (
    -1.0,
    -0.6962,
    -0.5251,
    -0.3949,
    -0.2844,
    -0.1848,
    -0.0911,
    0.0,
    0.0796,
    0.1609,
    0.2461,
    0.3379,
    0.4407,
    0.5626,
    0.723,
    1.0,
)
adapter_scale = 2.0
beta_one = 0.9
beta_two = 0.999
adam_step = 10.0
learn_rate = 0.05
decay_rate = 0.01
adam_eps = 1e-08
inverse_width = 1.0 / math.sqrt(MODEL_WIDTH)
coefficient = adapter_scale / math.sqrt(ADAPTER_RANK)


def flat_index(y, z, c, x):
    return ((y * NZ + z) * NC + c) * NX + x


def routed(value, route):
    pairs = []
    for y in range(NY):
        for z in range(NZ):
            for c in range(NC):
                for x in range(NX):
                    pairs.append((flat_index(y, z, c, x), flat_index(*route(y, z, c, x))))
    return lax.ppermute(value, ("fsdp", "tensor"), pairs)


def swap_cores(value):
    return routed(value, lambda y, z, c, x: (y, z, 1 - c, x))


def along_z(value, k):
    return routed(value, lambda y, z, c, x: (y, (z + k) % NZ, c, x))


def along_y(value, k):
    return routed(value, lambda y, z, c, x: ((y + k) % NY, z, c, x))


def along_x(value, k):
    return routed(value, lambda y, z, c, x: (y, z, c, (x + k) % NX))


def to_width_plane(value):
    return routed(value, lambda y, z, c, x: (x, (z % 4) * 2 + c, z // 4, y))


def adam_update(param, grad, moment, second):
    new_moment = beta_one * moment + (1.0 - beta_one) * grad
    new_second = beta_two * second + (1.0 - beta_two) * grad * grad
    corrected = new_moment / (1.0 - beta_one**adam_step)
    divisor = jnp.sqrt(new_second / (1.0 - beta_two**adam_step)) + adam_eps
    new_param = param - learn_rate * (corrected / divisor + decay_rate * param)
    return (new_param, new_moment, new_second)


def dequantize(quant_codes, block_scales):
    levels_out = jnp.zeros(quant_codes.shape, jnp.float32)
    for position in range(16):
        levels_out = jnp.where(quant_codes == position, nf4_levels[position], levels_out)
    row_count, col_count = quant_codes.shape
    blocks = block_scales.shape[1]
    scaled = levels_out.reshape(row_count, blocks, col_count // blocks) * block_scales[:, :, None]
    return scaled.reshape(row_count, col_count).astype(jnp.bfloat16)


def dot_nt(a, b):
    return lax.dot_general(a, b, (((1,), (1,)), ((), ())), preferred_element_type=jnp.float32)


def dot_nn(a, b):
    return lax.dot_general(a, b, (((1,), (0,)), ((), ())), preferred_element_type=jnp.float32)


def dot_tn(a, b):
    return lax.dot_general(a, b, (((0,), (0,)), ((), ())), preferred_element_type=jnp.float32)


def slot_of(info, jy, jz, kc):
    y, z, c = info[0], info[1], info[2]
    return ((y - jy) & 3) * 16 + ((z - jz) & 7) * 2 + (c ^ kc)


def spread_rows(info, slots, low, jy):
    rows = []
    for jz in range(NZ):
        for kc in range(NC):
            hit = slots == slot_of(info, jy, jz, kc)
            rows.append(jnp.where(hit, low, jnp.zeros_like(low)))
    return jnp.concatenate(rows, axis=0).astype(jnp.bfloat16)


def scores_body(info, slots_ref, x0, x1, d0, d1, a0, a1, a2, a3, out):
    half = x0.shape[1]
    toks = x0.shape[0]
    for h, (xr, dr) in enumerate(((x0, d0), (x1, d1))):
        slots = slots_ref[:, h * toks : (h + 1) * toks]
        in_sum = jnp.zeros((16, toks), jnp.float32)
        grad_sum = jnp.zeros((16, toks), jnp.float32)
        for jy, a in enumerate((a0, a1, a2, a3)):
            down = dot_nt(a[:, :half], xr[...])
            up = dot_nt(a[:, half:], dr[...])
            b = 0
            for jz in range(NZ):
                for kc in range(NC):
                    hit = slots == slot_of(info, jy, jz, kc)
                    in_sum = in_sum + jnp.where(hit, down[b : b + 16], 0.0)
                    grad_sum = grad_sum + jnp.where(hit, up[b : b + 16], 0.0)
                    b += 16
        out[0:16, h * toks : (h + 1) * toks] = in_sum * inverse_width
        out[16:32, h * toks : (h + 1) * toks] = grad_sum * coefficient


def terms_body(info, slots_ref, low_ref, x0, x1, d0, d1, *outs):
    half = x0.shape[1]
    toks = x0.shape[0]
    for jy, out in enumerate(outs):
        spreads_in, spreads_grad = [], []
        for h in range(2):
            cols = slice(h * toks, (h + 1) * toks)
            slots = slots_ref[:, cols]
            low = low_ref[:, cols].astype(jnp.float32)
            spreads_in.append(spread_rows(info, slots, low[0:16], jy))
            spreads_grad.append(spread_rows(info, slots, low[16:32], jy))
        down = dot_nn(spreads_grad[0], x0[...]) + dot_nn(spreads_grad[1], x1[...])
        out[:, :half] = (down * inverse_width).astype(jnp.bfloat16)
        up = dot_nn(spreads_in[0], d0[...]) + dot_nn(spreads_in[1], d1[...])
        out[:, half:] = (up * coefficient).astype(jnp.bfloat16)


def sum_split_body(r0, r1, r2, r3, *outs):
    rows = outs[0].shape[0]
    for j, out in enumerate(outs):
        at = slice(j * rows, (j + 1) * rows)
        total = r0[at, :].astype(jnp.float32) + r1[at, :].astype(jnp.float32)
        total = total + r2[at, :].astype(jnp.float32) + r3[at, :].astype(jnp.float32)
        out[...] = total.astype(jnp.bfloat16)


def product_body(info, slots_ref, low_ref, dv, a0, a1, a2, a3, w0, w1, w2, w3, w4a, w4b, w5, w6, w7, o0, o1, acc):
    toks, half = o0.shape
    x, y, z = info[3], info[0], info[1]
    for h, out in enumerate((o0, o1)):
        cols = slice(h * toks, (h + 1) * toks)
        slots = slots_ref[:, cols]
        low = low_ref[16:32, cols].astype(jnp.float32)
        total = jnp.zeros((toks, half), jnp.float32)
        for jy, a in enumerate((a0, a1, a2, a3)):
            total = total + dot_tn(spread_rows(info, slots, low, jy), a[:, :half])
        acc[...] = total * inverse_width
        for j, blocks in enumerate((w0, w1, w2, w3, (w4a, w4b), w5, w6, w7)):
            at = pl.ds(pl.multiple_of(((z - j) & 7) * 128, 128), 128)
            part = acc[:, at]
            for q in range(NY):
                if j == 4:
                    w = blocks[q // 2][q % 2]
                else:
                    w = blocks[q]
                part = part + dot_nt(dv[(x - y + q) & 3, cols, :], w)
            out[:, at] = part.astype(jnp.bfloat16)


def in_vmem(count):
    return [pl.BlockSpec(memory_space=pltpu.VMEM)] * count


SCALARS = pl.BlockSpec(memory_space=pltpu.SMEM)


def shape_of(shape, dtype):
    return jax.ShapeDtypeStruct(shape, dtype)


def call(body, name, operands, outs, flops, scalars=True, scratch=()):
    vmem_count = len(operands) - (1 if scalars else 0)
    specs = ([SCALARS] if scalars else []) + in_vmem(vmem_count)
    moved = sum(o.size * o.dtype.itemsize for o in operands)
    moved += sum(math.prod(o.shape) * jnp.dtype(o.dtype).itemsize for o in outs)
    return pl.pallas_call(
        body,
        out_shape=outs,
        in_specs=specs,
        out_specs=in_vmem(len(outs)),
        scratch_shapes=list(scratch),
        name=name,
        cost_estimate=pl.CostEstimate(flops=flops, bytes_accessed=moved, transcendentals=0),
    )(*operands)


def shards(
    layer_input,
    value_grad,
    quant_codes,
    block_scales,
    tenant_ids,
    live_counts,
    tenant_owner,
    factor_down,
    factor_up,
    moment_down,
    second_down,
    moment_up,
    second_up,
):
    toks, width = layer_input.shape
    values = value_grad.shape[1]
    half, vhalf = width // 2, values // 2
    seqs = tenant_ids.shape[0]
    seq_len = toks // seqs
    place = lax.axis_index("fsdp") * NX + lax.axis_index("tensor")
    info = (place // jnp.array([64, 8, 4, 1], jnp.int32)) % jnp.array([4, 8, 2, 4], jnp.int32)
    first = (place // 4) % 2 == 0

    def mine(a, n):
        return jnp.where(first, a[..., :n], a[..., n:])

    def theirs(a, n):
        return jnp.where(first, a[..., n:], a[..., :n])

    def joined(own, other):
        low = jnp.where(first, own, other)
        high = jnp.where(first, other, own)
        return jnp.concatenate([low, high], axis=-1)

    down_low = factor_down[0].astype(jnp.bfloat16)
    up_low = factor_up[0].astype(jnp.bfloat16)
    ab_own = jnp.concatenate([mine(down_low, half), mine(up_low, vhalf)], axis=1)
    ab_send = jnp.concatenate([theirs(down_low, half), theirs(up_low, vhalf)], axis=1)
    ab = jnp.concatenate([ab_own, swap_cores(ab_send)], axis=0)
    az = jnp.concatenate([ab] + [along_z(ab, j) for j in range(1, NZ)], axis=0)
    adapters = [az] + [along_y(az, j) for j in range(1, NY)]

    matches = tenant_ids[:, None] == jnp.arange(tenant_owner.shape[0], dtype=jnp.int32)[None, :]
    slot_own = jnp.sum(jnp.where(matches, tenant_owner[None, :], 0), axis=1)
    slot_all = jnp.concatenate([slot_own, swap_cores(slot_own)])
    slots = jnp.broadcast_to(slot_all[:, None], (2 * seqs, seq_len)).reshape(1, 2 * toks)
    live_tok = jnp.arange(toks, dtype=jnp.int32) // seq_len < live_counts[0]
    masked = jnp.where(live_tok[:, None], value_grad, jnp.zeros_like(value_grad))
    masked_other = swap_cores(masked)
    d0, d1 = mine(masked, vhalf), mine(masked_other, vhalf)
    x0 = mine(layer_input, half)
    x1 = swap_cores(theirs(layer_input, half))

    weight = to_width_plane(dequantize(quant_codes, block_scales))
    w0 = jnp.stack([weight] + [along_y(weight, j) for j in range(1, NY)])
    w1, w7 = along_z(w0, 1), along_z(w0, -1)
    w2, w6 = along_z(w1, 1), along_z(w7, -1)
    w3, w5 = along_z(w2, 1), along_z(w6, -1)
    w4a, w4b = along_z(w3[:2], 1), along_z(w5[2:], -1)
    chip_grad = jnp.concatenate([masked, masked_other], axis=0)
    dv = jnp.stack([chip_grad] + [along_x(chip_grad, j) for j in range(1, NX)])

    part = call(
        scores_body,
        "scores",
        (info, slots, x0, x1, d0, d1, *adapters),
        [shape_of((32, 2 * toks), jnp.float32)],
        2 * 2 * toks * 1024 * (half + vhalf),
    )[0]
    pair = part[:, :toks] + swap_cores(part[:, toks:])
    low = pair
    for j in range(1, NX):
        low = low + along_x(pair, j)
    low = low.astype(jnp.bfloat16)
    low = jnp.concatenate([low, swap_cores(low)], axis=1)

    rows = NZ * NC * ADAPTER_RANK
    terms = call(
        terms_body,
        "terms",
        (info, slots, low, x0, x1, d0, d1),
        [shape_of((rows, half + vhalf), jnp.bfloat16)] * NY,
        2 * 2 * toks * 1024 * (half + vhalf),
    )
    arrived = [terms[0]] + [along_y(terms[j], -j) for j in range(1, NY)]
    pieces = call(
        sum_split_body,
        "y_sums",
        tuple(arrived),
        [shape_of((NC * ADAPTER_RANK, half + vhalf), jnp.bfloat16)] * NZ,
        4 * rows * (half + vhalf),
        scalars=False,
    )
    total = pieces[0].astype(jnp.float32)
    for j in range(1, NZ):
        total = total + along_z(pieces[j], -j).astype(jnp.float32)
    own, other = total[:ADAPTER_RANK], swap_cores(total[ADAPTER_RANK:])
    down_gradient = joined(own[:, :half], other[:, :half])[None]
    up_gradient = joined(own[:, half:], other[:, half:])[None]
    new_down, new_moment_down, new_second_down = adam_update(
        factor_down, down_gradient, moment_down, second_down
    )
    new_up, new_moment_up, new_second_up = adam_update(factor_up, up_gradient, moment_up, second_up)

    o0, o1 = call(
        product_body,
        "product",
        (info, slots, low, dv, *adapters, w0, w1, w2, w3, w4a, w4b, w5, w6, w7),
        [shape_of((toks, half), jnp.bfloat16)] * 2,
        2 * 2 * toks * half * 2048,
        scratch=[pltpu.VMEM((toks, half), jnp.float32)],
    )
    layer_input_gradient = joined(o0, swap_cores(o1))
    return (
        layer_input_gradient,
        new_down,
        new_up,
        new_moment_down,
        new_second_down,
        new_moment_up,
        new_second_up,
    )


def solution(mesh):
    in_specs = (
        P("fsdp", "tensor"),
        P("fsdp", "tensor"),
        P("fsdp", "tensor"),
        P("fsdp", "tensor"),
        P("fsdp"),
        P("fsdp"),
        P(),
        P("fsdp", None, "tensor"),
        P("fsdp", None, "tensor"),
        P("fsdp", None, "tensor"),
        P("fsdp", None, "tensor"),
        P("fsdp", None, "tensor"),
        P("fsdp", None, "tensor"),
    )
    out_specs = (
        P("fsdp", "tensor"),
        P("fsdp", None, "tensor"),
        P("fsdp", None, "tensor"),
        P("fsdp", None, "tensor"),
        P("fsdp", None, "tensor"),
        P("fsdp", None, "tensor"),
        P("fsdp", None, "tensor"),
    )
    return jax.shard_map(shards, mesh=mesh, in_specs=in_specs, out_specs=out_specs, check_vma=False)
```

```python
import math

import jax
import jax.numpy as jnp
from jax import lax
from jax.experimental import pallas as pl
from jax.experimental.pallas import tpu as pltpu
from jax.sharding import PartitionSpec as P

MODEL_WIDTH = 8192
ADAPTER_RANK = 16
NY, NZ, NC, NX = 4, 8, 2, 4


nf4_levels = (
    -1.0,
    -0.6962,
    -0.5251,
    -0.3949,
    -0.2844,
    -0.1848,
    -0.0911,
    0.0,
    0.0796,
    0.1609,
    0.2461,
    0.3379,
    0.4407,
    0.5626,
    0.723,
    1.0,
)
adapter_scale = 2.0
beta_one = 0.9
beta_two = 0.999
adam_step = 10.0
learn_rate = 0.05
decay_rate = 0.01
adam_eps = 1e-08
inverse_width = 1.0 / math.sqrt(MODEL_WIDTH)
coefficient = adapter_scale / math.sqrt(ADAPTER_RANK)


def flat_index(y, z, c, x):
    return ((y * NZ + z) * NC + c) * NX + x


def routed(value, route):
    pairs = []
    for y in range(NY):
        for z in range(NZ):
            for c in range(NC):
                for x in range(NX):
                    pairs.append((flat_index(y, z, c, x), flat_index(*route(y, z, c, x))))
    return lax.ppermute(value, ("fsdp", "tensor"), pairs)


def swap_cores(value):
    return routed(value, lambda y, z, c, x: (y, z, 1 - c, x))


def both_ways_z(value, k):
    return routed(value, lambda y, z, c, x: (y, (z + (k if c == 0 else -k)) % NZ, c, x))


def along_y(value, k):
    return routed(value, lambda y, z, c, x: ((y + k) % NY, z, c, x))


def along_x(value, k):
    return routed(value, lambda y, z, c, x: (y, z, c, (x + k) % NX))


def to_width_plane(value):
    return routed(value, lambda y, z, c, x: (x, z, c, y))


def adam_update(param, grad, moment, second):
    new_moment = beta_one * moment + (1.0 - beta_one) * grad
    new_second = beta_two * second + (1.0 - beta_two) * grad * grad
    corrected = new_moment / (1.0 - beta_one**adam_step)
    divisor = jnp.sqrt(new_second / (1.0 - beta_two**adam_step)) + adam_eps
    new_param = param - learn_rate * (corrected / divisor + decay_rate * param)
    return (new_param, new_moment, new_second)


def dequantize(quant_codes, block_scales):
    levels_out = jnp.zeros(quant_codes.shape, jnp.float32)
    for position in range(16):
        levels_out = jnp.where(quant_codes == position, nf4_levels[position], levels_out)
    row_count, col_count = quant_codes.shape
    blocks = block_scales.shape[1]
    scaled = levels_out.reshape(row_count, blocks, col_count // blocks) * block_scales[:, :, None]
    return scaled.reshape(row_count, col_count).astype(jnp.bfloat16)


def dot_nt(a, b):
    return lax.dot_general(a, b, (((1,), (1,)), ((), ())), preferred_element_type=jnp.float32)


def dot_nn(a, b):
    return lax.dot_general(a, b, (((1,), (0,)), ((), ())), preferred_element_type=jnp.float32)


PIECES = ((0, None), (1, 0), (1, 1), (2, 0), (2, 1), (3, 0), (3, 1), (4, None))


def chip_at(info, core, step):
    z = info[1]
    return jnp.where(core == 0, z - step, z + step) & 7


def block_of(info, core, piece):
    step, a = PIECES[piece]
    return chip_at(info, core, step) * 2 + (core if a is None else a)


def spread_rows(info, slots, low, jy):
    y, c = info[0], info[2]
    rows = []
    for piece in range(8):
        hit = slots == ((y - jy) & 3) * 16 + block_of(info, c, piece)
        rows.append(jnp.where(hit, low, jnp.zeros_like(low)))
    return jnp.concatenate(rows, axis=0)


def scores_body(info, slots_ref, x0, x1, d0, d1, a0, a1, a2, a3, out, acc):
    toks, width = x0.shape
    y, c = info[0], info[2]
    adapters = (a0, a1, a2, a3)
    for h, (xr, dr) in enumerate(((x0, d0), (x1, d1))):
        slots = slots_ref[:, h * toks : (h + 1) * toks]
        acc[1] = dot_nt(jnp.concatenate([a[:, width:] for a in adapters], axis=0), dr[...])
        acc[0] = jnp.zeros((512, toks), jnp.float32)

        @pl.loop(0, 2)
        def _(k, xr=xr):
            at = pl.ds(pl.multiple_of(k * 1024, 1024), 1024)
            acc[0] += dot_nt(jnp.concatenate([a[:, at] for a in adapters], axis=0), xr[:, at])

        in_sum = jnp.zeros((16, toks), jnp.float32)
        grad_sum = jnp.zeros((16, toks), jnp.float32)
        for jy in range(NY):
            for piece in range(8):
                hit = slots == ((y - jy) & 3) * 16 + block_of(info, c, piece)
                rows = slice(jy * 128 + piece * 16, jy * 128 + piece * 16 + 16)
                in_sum = in_sum + jnp.where(hit, acc[0, rows, :], 0.0)
                grad_sum = grad_sum + jnp.where(hit, acc[1, rows, :], 0.0)
        out[0:16, h * toks : (h + 1) * toks] = in_sum * inverse_width
        out[16:32, h * toks : (h + 1) * toks] = grad_sum * coefficient


def terms_body(info, slots_ref, low_ref, x0, x1, d0, d1, o0, o1, o2, o3, sg, si):
    toks, width = x0.shape
    outs = (o0, o1, o2, o3)
    for h in range(2):
        cols = slice(h * toks, (h + 1) * toks)
        slots = slots_ref[:, cols]
        low = low_ref[:, cols].astype(jnp.float32)
        for jy in range(NY):
            rows = slice(jy * 128, (jy + 1) * 128)
            sg[h, rows, :] = spread_rows(info, slots, low[16:32], jy).astype(jnp.bfloat16)
            si[h, rows, :] = spread_rows(info, slots, low[0:16], jy).astype(jnp.bfloat16)

    @pl.loop(0, width // 256)
    def _(k):
        at = pl.ds(pl.multiple_of(k * 256, 256), 256)
        down = dot_nn(sg[0], x0[:, at]) + dot_nn(sg[1], x1[:, at])
        down = (down * inverse_width).astype(jnp.bfloat16)
        for jy, out in enumerate(outs):
            out[:, at] = down[jy * 128 : (jy + 1) * 128]

    up = dot_nn(si[0], d0[...]) + dot_nn(si[1], d1[...])
    up = (up * coefficient).astype(jnp.bfloat16)
    for jy, out in enumerate(outs):
        out[:, width:] = up[jy * 128 : (jy + 1) * 128]


def y_sums_body(r0, r1, r2, r3, o0, o1, o2, o3, o4):
    at = 0
    for out in (o0, o1, o2, o3, o4):
        rows = slice(at, at + out.shape[0])
        total = r0[rows, :].astype(jnp.float32) + r1[rows, :].astype(jnp.float32)
        total = total + r2[rows, :].astype(jnp.float32) + r3[rows, :].astype(jnp.float32)
        out[...] = total.astype(out.dtype)
        at += out.shape[0]


def z_sums_body(info, p0, r1, r2, r3, r4, own, other):
    c = info[2]
    mine = pl.ds(pl.multiple_of(c * 16, 16), 16)
    theirs = pl.ds(pl.multiple_of((1 - c) * 16, 16), 16)
    total = p0[...] + r4[...].astype(jnp.float32)
    for r in (r1, r2, r3):
        total = total + r[mine, :].astype(jnp.float32)
    own[...] = total
    total = r1[theirs, :].astype(jnp.float32) + r2[theirs, :].astype(jnp.float32)
    other[...] = total + r3[theirs, :].astype(jnp.float32)


def back_body(info, slots_ref, low_ref, a0, a1, a2, a3, keep, send, spread, by_step):
    toks = slots_ref.shape[1] // 2
    c = info[2]
    for h in range(2):
        cols = slice(h * toks, (h + 1) * toks)
        slots = slots_ref[:, cols]
        low = low_ref[16:32, cols].astype(jnp.float32)
        for jy in range(NY):
            turned = spread_rows(info, slots, low, jy).T
            spread[cols, jy * 128 : (jy + 1) * 128] = turned.astype(jnp.bfloat16)

    @pl.loop(0, NZ)
    def _(step):
        at = pl.ds(pl.multiple_of(chip_at(info, c, step) * 256, 256), 256)
        part = jnp.concatenate([a[:, at] for a in (a0, a1, a2, a3)], axis=0)
        by_step[step] = (dot_nn(spread[...], part) * inverse_width).astype(jnp.bfloat16)

    for piece, (step, a) in enumerate(PIECES):
        to = slice(piece * 128, (piece + 1) * 128)
        if a is None:
            first, second = by_step[step, :, :128], by_step[step, :, 128:]
            keep[:, to] = jnp.where(c == 0, first, second)
            send[:, to] = jnp.where(c == 0, second, first)
        else:
            keep[:, to] = by_step[step, :, a * 128 : (a + 1) * 128]
            send[:, to] = by_step[8 - step, :, a * 128 : (a + 1) * 128]


def base_body(info, dv, *refs):
    y, x = info[0], info[3]
    *weights, out = refs
    out[...] = jnp.zeros_like(out)

    @pl.loop(0, NY)
    def _(q):
        grads = dv[(x - y + q) & 3]
        at = 0
        for w in weights:
            rows = w[q] if len(w.shape) == 3 else jnp.concatenate([w[0, q], w[1, q]], axis=0)
            out[:, at : at + rows.shape[0]] += dot_nt(grads, rows)
            at += rows.shape[0]


def finish_body(info, dv, w4, b01, b2, b3, keep, came, o0, o1, acc):
    toks = o0.shape[0]
    base_body(info, dv, w4, acc)
    for h, out in enumerate((o0, o1)):
        rows = slice(h * toks, (h + 1) * toks)
        turned = slice((1 - h) * toks, (2 - h) * toks)
        at = 0
        for base in (b01, b2, b3, acc):
            cols = slice(at, at + base.shape[1])
            total = base[rows, :] + keep[rows, cols].astype(jnp.float32)
            total = total + came[turned, cols].astype(jnp.float32)
            out[:, cols] = total.astype(jnp.bfloat16)
            at += base.shape[1]


def place_body(info, own, other, out):
    c = info[2]
    for core, ref in ((c, own), (1 - c, other)):
        for piece in range(8):
            at = pl.multiple_of(block_of(info, core, piece) * 128, 128)
            out[:, pl.ds(at, 128)] = ref[:, piece * 128 : (piece + 1) * 128]


SCALARS = pl.BlockSpec(memory_space=pltpu.SMEM)
LOCAL = pl.BlockSpec(memory_space=pltpu.VMEM)


def shape_of(shape, dtype):
    return jax.ShapeDtypeStruct(shape, dtype)


def call(body, operands, outs, flops, scalars=True, scratch=()):
    vmem_count = len(operands) - (1 if scalars else 0)
    moved = sum(o.size * o.dtype.itemsize for o in operands)
    moved += sum(math.prod(o.shape) * jnp.dtype(o.dtype).itemsize for o in outs)
    return pl.pallas_call(
        body,
        out_shape=outs,
        in_specs=([SCALARS] if scalars else []) + [LOCAL] * vmem_count,
        out_specs=[LOCAL] * len(outs),
        scratch_shapes=list(scratch),
        compiler_params=pltpu.CompilerParams(vmem_limit_bytes=24 * 1024 * 1024),
        cost_estimate=pl.CostEstimate(flops=flops, bytes_accessed=moved, transcendentals=0),
    )(*operands)


def shards(
    layer_input,
    value_grad,
    quant_codes,
    block_scales,
    tenant_ids,
    live_counts,
    tenant_owner,
    factor_down,
    factor_up,
    moment_down,
    second_down,
    moment_up,
    second_up,
):
    toks, width = layer_input.shape
    values = value_grad.shape[1]
    wide = width + values
    half = width // 2
    seqs = tenant_ids.shape[0]
    seq_len = toks // seqs
    place = lax.axis_index("fsdp") * NX + lax.axis_index("tensor")
    info = (place // jnp.array([64, 8, 4, 1], jnp.int32)) % jnp.array([4, 8, 2, 4], jnp.int32)
    first = (place // 4) % 2 == 0

    def in_order(own, other, axis=0):
        low = jnp.where(first, own, other)
        high = jnp.where(first, other, own)
        return jnp.concatenate([low, high], axis=axis)

    ab = jnp.concatenate([factor_down[0], factor_up[0]], axis=1).astype(jnp.bfloat16)
    chip_ab = in_order(ab, swap_cores(ab))
    steps = [both_ways_z(chip_ab, k) for k in range(1, 4)]
    az = jnp.concatenate([ab] + steps + [both_ways_z(ab, 4)], axis=0)
    adapters = [az] + [along_y(az, j) for j in range(1, NY)]

    matches = tenant_ids[:, None] == jnp.arange(tenant_owner.shape[0], dtype=jnp.int32)[None, :]
    slot_own = jnp.sum(jnp.where(matches, tenant_owner[None, :], 0), axis=1)
    slot_all = jnp.concatenate([slot_own, swap_cores(slot_own)])
    slots = jnp.broadcast_to(slot_all[:, None], (2 * seqs, seq_len)).reshape(1, 2 * toks)
    live_tok = jnp.arange(toks, dtype=jnp.int32) // seq_len < live_counts[0]
    d0 = jnp.where(live_tok[:, None], value_grad, jnp.zeros_like(value_grad))
    d1 = swap_cores(d0)
    x0, x1 = layer_input, swap_cores(layer_input)

    weight = to_width_plane(dequantize(quant_codes, block_scales))
    w0 = jnp.stack([weight] + [along_y(weight, j) for j in range(1, NY)])
    w1 = both_ways_z(in_order(w0[None], swap_cores(w0)[None]), 1)
    w2 = both_ways_z(w1, 1)
    w3 = both_ways_z(w2, 1)
    w4 = both_ways_z(jnp.where(first, w3[0], w3[1]), 1)
    chip_grad = jnp.concatenate([d0, d1], axis=0)
    dv = jnp.stack([chip_grad] + [along_x(chip_grad, j) for j in range(1, NX)])

    def base(*weights):
        columns = sum(w.size // 1024 for w in weights)
        return call(
            base_body,
            (info, dv, *weights),
            [shape_of((2 * toks, columns), jnp.float32)],
            2 * 2 * toks * columns * 1024,
        )[0]

    b01, b2, b3 = base(w0, w1), base(w2), base(w3)

    part = call(
        scores_body,
        (info, slots, x0, x1, d0, d1, *adapters),
        [shape_of((32, 2 * toks), jnp.float32)],
        2 * 2 * toks * 512 * wide,
        scratch=[pltpu.VMEM((2, 512, toks), jnp.float32)],
    )[0]
    pair = part[:, :toks] + swap_cores(part[:, toks:])
    low = pair
    for j in range(1, NX):
        low = low + along_x(pair, j)
    low = low.astype(jnp.bfloat16)
    low = jnp.concatenate([low, swap_cores(low)], axis=1)

    spread = pltpu.VMEM((2, 512, toks), jnp.bfloat16)
    terms = call(
        terms_body,
        (info, slots, low, x0, x1, d0, d1),
        [shape_of((128, wide), jnp.bfloat16)] * NY,
        2 * 2 * toks * 512 * wide,
        scratch=[spread, spread],
    )
    arrived = [terms[0]] + [along_y(terms[j], -j) for j in range(1, NY)]
    pieces = call(
        y_sums_body,
        tuple(arrived),
        [shape_of((16, wide), jnp.float32)]
        + [shape_of((32, wide), jnp.bfloat16)] * 3
        + [shape_of((16, wide), jnp.bfloat16)],
        4 * 128 * wide,
        scalars=False,
    )
    came = [both_ways_z(pieces[k], -k) for k in range(1, 5)]
    own, other = call(
        z_sums_body,
        (info, pieces[0], *came),
        [shape_of((16, wide), jnp.float32)] * 2,
        8 * 16 * wide,
    )
    gradient = own + swap_cores(other)
    down_gradient, up_gradient = gradient[None, :, :width], gradient[None, :, width:]
    new_down, new_moment_down, new_second_down = adam_update(
        factor_down, down_gradient, moment_down, second_down
    )
    new_up, new_moment_up, new_second_up = adam_update(factor_up, up_gradient, moment_up, second_up)

    keep, send = call(
        back_body,
        (info, slots, low, *adapters),
        [shape_of((2 * toks, half), jnp.bfloat16)] * 2,
        2 * 2 * toks * 512 * width,
        scratch=[
            pltpu.VMEM((2 * toks, 512), jnp.bfloat16),
            pltpu.VMEM((NZ, 2 * toks, 256), jnp.bfloat16),
        ],
    )
    o0, o1 = call(
        finish_body,
        (info, dv, w4, b01, b2, b3, keep, swap_cores(send)),
        [shape_of((toks, half), jnp.bfloat16)] * 2,
        2 * 2 * toks * 128 * 1024,
        scratch=[pltpu.VMEM((2 * toks, 128), jnp.float32)],
    )
    layer_input_gradient = call(
        place_body, (info, o0, swap_cores(o1)), [shape_of((toks, width), jnp.bfloat16)], 0
    )[0]
    return (
        layer_input_gradient,
        new_down,
        new_up,
        new_moment_down,
        new_second_down,
        new_moment_up,
        new_second_up,
    )


def solution(mesh):
    in_specs = (
        P("fsdp", "tensor"),
        P("fsdp", "tensor"),
        P("fsdp", "tensor"),
        P("fsdp", "tensor"),
        P("fsdp"),
        P("fsdp"),
        P(),
        P("fsdp", None, "tensor"),
        P("fsdp", None, "tensor"),
        P("fsdp", None, "tensor"),
        P("fsdp", None, "tensor"),
        P("fsdp", None, "tensor"),
        P("fsdp", None, "tensor"),
    )
    out_specs = (
        P("fsdp", "tensor"),
        P("fsdp", None, "tensor"),
        P("fsdp", None, "tensor"),
        P("fsdp", None, "tensor"),
        P("fsdp", None, "tensor"),
        P("fsdp", None, "tensor"),
        P("fsdp", None, "tensor"),
    )

    return jax.shard_map(shards, mesh=mesh, in_specs=in_specs, out_specs=out_specs, check_vma=False)
```

```python
import math

import jax
import jax.numpy as jnp
from jax import lax
from jax.experimental import pallas as pl
from jax.experimental.pallas import tpu as pltpu
from jax.sharding import PartitionSpec as P

MODEL_WIDTH = 8192
ADAPTER_RANK = 16
NY, NZ, NC, NX = 4, 8, 2, 4


nf4_levels = (
    -1.0,
    -0.6962,
    -0.5251,
    -0.3949,
    -0.2844,
    -0.1848,
    -0.0911,
    0.0,
    0.0796,
    0.1609,
    0.2461,
    0.3379,
    0.4407,
    0.5626,
    0.723,
    1.0,
)
adapter_scale = 2.0
beta_one = 0.9
beta_two = 0.999
adam_step = 10.0
learn_rate = 0.05
decay_rate = 0.01
adam_eps = 1e-08
inverse_width = 1.0 / math.sqrt(MODEL_WIDTH)
coefficient = adapter_scale / math.sqrt(ADAPTER_RANK)


def flat_index(y, z, c, x):
    return ((y * NZ + z) * NC + c) * NX + x


def routed(value, route):
    pairs = []
    for y in range(NY):
        for z in range(NZ):
            for c in range(NC):
                for x in range(NX):
                    pairs.append((flat_index(y, z, c, x), flat_index(*route(y, z, c, x))))
    return lax.ppermute(value, ("fsdp", "tensor"), pairs)


def swap_cores(value):
    return routed(value, lambda y, z, c, x: (y, z, 1 - c, x))


def both_ways_z(value, k):
    return routed(value, lambda y, z, c, x: (y, (z + (k if c == 0 else -k)) % NZ, c, x))


def along_y(value, k):
    return routed(value, lambda y, z, c, x: ((y + k) % NY, z, c, x))


def along_x(value, k):
    return routed(value, lambda y, z, c, x: (y, z, c, (x + k) % NX))


def to_width_plane(value):
    return routed(value, lambda y, z, c, x: (x, z, c, y))


def adam_update(param, grad, moment, second):
    new_moment = beta_one * moment + (1.0 - beta_one) * grad
    new_second = beta_two * second + (1.0 - beta_two) * grad * grad
    corrected = new_moment / (1.0 - beta_one**adam_step)
    divisor = jnp.sqrt(new_second / (1.0 - beta_two**adam_step)) + adam_eps
    new_param = param - learn_rate * (corrected / divisor + decay_rate * param)
    return (new_param, new_moment, new_second)


def dequantize(quant_codes, block_scales):
    levels_out = jnp.zeros(quant_codes.shape, jnp.float32)
    for position in range(16):
        levels_out = jnp.where(quant_codes == position, nf4_levels[position], levels_out)
    row_count, col_count = quant_codes.shape
    blocks = block_scales.shape[1]
    scaled = levels_out.reshape(row_count, blocks, col_count // blocks) * block_scales[:, :, None]
    return scaled.reshape(row_count, col_count).astype(jnp.bfloat16)


def dot_nt(a, b):
    return lax.dot_general(a, b, (((1,), (1,)), ((), ())), preferred_element_type=jnp.float32)


def dot_nn(a, b):
    return lax.dot_general(a, b, (((1,), (0,)), ((), ())), preferred_element_type=jnp.float32)


PIECES = ((0, None), (1, 0), (1, 1), (2, 0), (2, 1), (3, 0), (3, 1), (4, None))


def chip_at(info, core, step):
    z = info[1]
    return jnp.where(core == 0, z - step, z + step) & 7


def block_of(info, core, piece):
    step, a = PIECES[piece]
    return chip_at(info, core, step) * 2 + (core if a is None else a)


def spread_rows(info, slots, low, jy):
    y, c = info[0], info[2]
    rows = []
    for piece in range(8):
        hit = slots == ((y - jy) & 3) * 16 + block_of(info, c, piece)
        rows.append(jnp.where(hit, low, jnp.zeros_like(low)))
    return jnp.concatenate(rows, axis=0)


def pick_rows(info, slots, scores):
    y, c = info[0], info[2]
    total = jnp.zeros((16, slots.shape[1]), jnp.float32)
    for jy in range(NY):
        for piece in range(8):
            hit = slots == ((y - jy) & 3) * 16 + block_of(info, c, piece)
            at = jy * 128 + piece * 16
            total = total + jnp.where(hit, scores[at : at + 16, :], 0.0)
    return total


def up_scores_body(info, slots_ref, d0, d1, b0, b1, b2, b3, out, turned, acc):
    toks = d0.shape[0]
    for h, dr in enumerate((d0, d1)):
        cols = slice(h * toks, (h + 1) * toks)
        acc[...] = dot_nt(jnp.concatenate([b[...] for b in (b0, b1, b2, b3)], axis=0), dr[...])
        total = pick_rows(info, slots_ref[:, cols], acc) * coefficient
        out[:, cols] = total
        turned[:, (1 - h) * toks : (2 - h) * toks] = total


def scores_body(info, slots_ref, x0, x1, a0, a1, a2, a3, out, turned, acc):
    toks = x0.shape[0]
    for h, xr in enumerate((x0, x1)):
        cols = slice(h * toks, (h + 1) * toks)
        acc[...] = jnp.zeros_like(acc)

        @pl.loop(0, 2)
        def _(k, xr=xr):
            at = pl.ds(pl.multiple_of(k * 1024, 1024), 1024)
            acc[...] += dot_nt(jnp.concatenate([a[:, at] for a in (a0, a1, a2, a3)], axis=0), xr[:, at])

        total = pick_rows(info, slots_ref[:, cols], acc) * inverse_width
        out[:, cols] = total
        turned[:, (1 - h) * toks : (2 - h) * toks] = total


def spread_all(info, slots_ref, low_ref, toks, spread):
    for h in range(2):
        cols = slice(h * toks, (h + 1) * toks)
        low = low_ref[:, cols].astype(jnp.float32)
        for jy in range(NY):
            rows = spread_rows(info, slots_ref[:, cols], low, jy)
            spread[h, jy * 128 : (jy + 1) * 128, :] = rows.astype(jnp.bfloat16)


def down_terms_body(info, slots_ref, low_ref, x0, x1, o0, o1, o2, o3, spread):
    toks, width = x0.shape
    spread_all(info, slots_ref, low_ref, toks, spread)

    @pl.loop(0, width // 256)
    def _(k):
        at = pl.ds(pl.multiple_of(k * 256, 256), 256)
        down = dot_nn(spread[0], x0[:, at]) + dot_nn(spread[1], x1[:, at])
        down = (down * inverse_width).astype(jnp.bfloat16)
        for jy, out in enumerate((o0, o1, o2, o3)):
            out[:, at] = down[jy * 128 : (jy + 1) * 128]


def up_terms_body(info, slots_ref, low_ref, d0, d1, o0, o1, o2, o3, spread):
    spread_all(info, slots_ref, low_ref, d0.shape[0], spread)
    up = dot_nn(spread[0], d0[...]) + dot_nn(spread[1], d1[...])
    up = (up * coefficient).astype(jnp.bfloat16)
    for jy, out in enumerate((o0, o1, o2, o3)):
        out[...] = up[jy * 128 : (jy + 1) * 128]


def y_sums_body(r0, r1, r2, r3, u0, u1, u2, u3, *outs):
    width = r0.shape[1]
    at = 0
    for out in outs:
        rows = slice(at, at + out.shape[0])
        total = r0[rows, :].astype(jnp.float32) + r1[rows, :].astype(jnp.float32)
        total = total + r2[rows, :].astype(jnp.float32) + r3[rows, :].astype(jnp.float32)
        out[:, :width] = total.astype(out.dtype)
        total = u0[rows, :].astype(jnp.float32) + u1[rows, :].astype(jnp.float32)
        total = total + u2[rows, :].astype(jnp.float32) + u3[rows, :].astype(jnp.float32)
        out[:, width:] = total.astype(out.dtype)
        at += out.shape[0]


def z_sums_body(info, p0, r1, r2, r3, r4, own, other):
    c = info[2]
    mine = pl.ds(pl.multiple_of(c * 16, 16), 16)
    theirs = pl.ds(pl.multiple_of((1 - c) * 16, 16), 16)
    total = p0[...] + r4[...].astype(jnp.float32)
    for r in (r1, r2, r3):
        total = total + r[mine, :].astype(jnp.float32)
    own[...] = total
    total = r1[theirs, :].astype(jnp.float32) + r2[theirs, :].astype(jnp.float32)
    other[...] = total + r3[theirs, :].astype(jnp.float32)


def back_body(info, slots_ref, low_ref, a0, a1, a2, a3, keep, send, spread, by_step):
    toks = slots_ref.shape[1] // 2
    c = info[2]
    for h in range(2):
        cols = slice(h * toks, (h + 1) * toks)
        slots = slots_ref[:, cols]
        low = low_ref[:, cols].astype(jnp.float32)
        for jy in range(NY):
            turned = spread_rows(info, slots, low, jy).T
            spread[cols, jy * 128 : (jy + 1) * 128] = turned.astype(jnp.bfloat16)

    @pl.loop(0, NZ)
    def _(step):
        at = pl.ds(pl.multiple_of(chip_at(info, c, step) * 256, 256), 256)
        part = jnp.concatenate([a[:, at] for a in (a0, a1, a2, a3)], axis=0)
        by_step[step] = (dot_nn(spread[...], part) * inverse_width).astype(jnp.bfloat16)

    for piece, (step, a) in enumerate(PIECES):
        to = slice(piece * 128, (piece + 1) * 128)
        if a is None:
            first, second = by_step[step, :, :128], by_step[step, :, 128:]
            keep[:, to] = jnp.where(c == 0, first, second)
            send[:, to] = jnp.where(c == 0, second, first)
        else:
            keep[:, to] = by_step[step, :, a * 128 : (a + 1) * 128]
            send[:, to] = by_step[8 - step, :, a * 128 : (a + 1) * 128]


def base_body(info, dv, *refs):
    y, x = info[0], info[3]
    *weights, out = refs
    out[...] = jnp.zeros_like(out)

    @pl.loop(0, NY)
    def _(q):
        grads = dv[(x - y + q) & 3]
        at = 0
        for w in weights:
            rows = w[q] if len(w.shape) == 3 else jnp.concatenate([w[0, q], w[1, q]], axis=0)
            out[:, at : at + rows.shape[0]] += dot_nt(grads, rows)
            at += rows.shape[0]


def finish_body(info, dv, w4, b01, b2, b3, keep, came, o0, o1, acc):
    toks = o0.shape[0]
    base_body(info, dv, w4, acc)
    for h, out in enumerate((o0, o1)):
        rows = slice(h * toks, (h + 1) * toks)
        turned = slice((1 - h) * toks, (2 - h) * toks)
        at = 0
        for base in (b01, b2, b3, acc):
            cols = slice(at, at + base.shape[1])
            total = base[rows, :] + keep[rows, cols].astype(jnp.float32)
            total = total + came[turned, cols].astype(jnp.float32)
            out[:, cols] = total.astype(jnp.bfloat16)
            at += base.shape[1]


def place_body(info, own, other, out):
    c = info[2]
    for core, ref in ((c, own), (1 - c, other)):
        for piece in range(8):
            at = pl.multiple_of(block_of(info, core, piece) * 128, 128)
            out[:, pl.ds(at, 128)] = ref[:, piece * 128 : (piece + 1) * 128]


SCALARS = pl.BlockSpec(memory_space=pltpu.SMEM)
LOCAL = pl.BlockSpec(memory_space=pltpu.VMEM)


def shape_of(shape, dtype):
    return jax.ShapeDtypeStruct(shape, dtype)


def call(body, operands, outs, flops, scalars=True, scratch=()):
    vmem_count = len(operands) - (1 if scalars else 0)
    moved = sum(o.size * o.dtype.itemsize for o in operands)
    moved += sum(math.prod(o.shape) * jnp.dtype(o.dtype).itemsize for o in outs)
    return pl.pallas_call(
        body,
        out_shape=outs,
        in_specs=([SCALARS] if scalars else []) + [LOCAL] * vmem_count,
        out_specs=[LOCAL] * len(outs),
        scratch_shapes=list(scratch),
        compiler_params=pltpu.CompilerParams(vmem_limit_bytes=24 * 1024 * 1024),
        cost_estimate=pl.CostEstimate(flops=flops, bytes_accessed=moved, transcendentals=0),
    )(*operands)


def shards(
    layer_input,
    value_grad,
    quant_codes,
    block_scales,
    tenant_ids,
    live_counts,
    tenant_owner,
    factor_down,
    factor_up,
    moment_down,
    second_down,
    moment_up,
    second_up,
):
    toks, width = layer_input.shape
    values = value_grad.shape[1]
    wide = width + values
    half = width // 2
    seqs = tenant_ids.shape[0]
    seq_len = toks // seqs
    place = lax.axis_index("fsdp") * NX + lax.axis_index("tensor")
    info = (place // jnp.array([64, 8, 4, 1], jnp.int32)) % jnp.array([4, 8, 2, 4], jnp.int32)
    first = (place // 4) % 2 == 0

    def in_order(own, other, axis=0):
        low = jnp.where(first, own, other)
        high = jnp.where(first, other, own)
        return jnp.concatenate([low, high], axis=axis)

    matches = tenant_ids[:, None] == jnp.arange(tenant_owner.shape[0], dtype=jnp.int32)[None, :]
    slot_own = jnp.sum(jnp.where(matches, tenant_owner[None, :], 0), axis=1)

    ab = jnp.concatenate([factor_down[0], factor_up[0]], axis=1).astype(jnp.bfloat16)
    riders = jnp.broadcast_to(slot_own.astype(jnp.bfloat16)[:, None], (seqs, 128))
    swapped = swap_cores(jnp.concatenate([ab, riders], axis=1))
    chip_ab = in_order(ab, swapped[:, :wide])
    slot_other = swapped[:, wide].astype(jnp.int32)
    steps = [both_ways_z(chip_ab, k) for k in range(1, 4)]
    steps = [ab] + steps + [both_ways_z(ab, 4)]
    bz = jnp.concatenate([s[:, width:] for s in steps], axis=0)
    az = jnp.concatenate([s[:, :width] for s in steps], axis=0)
    ups = [bz] + [along_y(bz, j) for j in range(1, NY)]
    downs = [az] + [along_y(az, j) for j in range(1, NY)]

    slot_all = jnp.concatenate([slot_own, slot_other])
    slots = jnp.broadcast_to(slot_all[:, None], (2 * seqs, seq_len)).reshape(1, 2 * toks)
    live_tok = jnp.arange(toks, dtype=jnp.int32) // seq_len < live_counts[0]
    d0 = jnp.where(live_tok[:, None], value_grad, jnp.zeros_like(value_grad))
    d1 = swap_cores(d0)
    x0, x1 = layer_input, swap_cores(layer_input)

    weight = to_width_plane(dequantize(quant_codes, block_scales))
    w0 = jnp.stack([weight] + [along_y(weight, j) for j in range(1, NY)])
    w1 = both_ways_z(in_order(w0[None], swap_cores(w0)[None]), 1)
    w2 = both_ways_z(w1, 1)
    w3 = both_ways_z(w2, 1)
    w4 = both_ways_z(jnp.where(first, w3[0], w3[1]), 1)
    chip_grad = jnp.concatenate([d0, d1], axis=0)
    dv = jnp.stack([chip_grad] + [along_x(chip_grad, j) for j in range(1, NX)])

    def base(*weights):
        columns = sum(w.size // 1024 for w in weights)
        return call(
            base_body,
            (info, dv, *weights),
            [shape_of((2 * toks, columns), jnp.float32)],
            2 * 2 * toks * columns * 1024,
        )[0]

    b01, b2, b3 = base(w0, w1), base(w2), base(w3)

    def rank_sums(body, operands, flops):
        own, turned = call(
            body,
            operands,
            [shape_of((ADAPTER_RANK, 2 * toks), jnp.float32)] * 2,
            flops,
            scratch=[pltpu.VMEM((512, toks), jnp.float32)],
        )
        pair = own + swap_cores(turned)
        total = pair
        for j in range(1, NX):
            total = total + along_x(pair, j)
        return total.astype(jnp.bfloat16)

    spread = pltpu.VMEM((2, 512, toks), jnp.bfloat16)
    rank_flops = 2 * 2 * toks * 512

    def row_terms(body, operands, columns):
        return call(
            body,
            operands,
            [shape_of((128, columns), jnp.bfloat16)] * NY,
            rank_flops * columns,
            scratch=[spread],
        )

    low = rank_sums(up_scores_body, (info, slots, d0, d1, *ups), rank_flops * values)
    terms = row_terms(down_terms_body, (info, slots, low, x0, x1), width)
    arrived = [terms[0]] + [along_y(terms[j], -j) for j in range(1, NY)]

    in_low = rank_sums(scores_body, (info, slots, x0, x1, *downs), rank_flops * width)
    terms = row_terms(up_terms_body, (info, slots, in_low, d0, d1), values)
    arrived += [terms[0]] + [along_y(terms[j], -j) for j in range(1, NY)]
    pieces = call(
        y_sums_body,
        tuple(arrived),
        [shape_of((16, wide), jnp.float32)]
        + [shape_of((32, wide), jnp.bfloat16)] * 3
        + [shape_of((16, wide), jnp.bfloat16)],
        4 * 128 * wide,
        scalars=False,
    )
    came = [both_ways_z(pieces[k], -k) for k in range(1, 5)]
    own, other = call(
        z_sums_body,
        (info, pieces[0], *came),
        [shape_of((16, wide), jnp.float32)] * 2,
        8 * 16 * wide,
    )
    gradient = own + swap_cores(other)
    down_gradient, up_gradient = gradient[None, :, :width], gradient[None, :, width:]
    new_down, new_moment_down, new_second_down = adam_update(
        factor_down, down_gradient, moment_down, second_down
    )
    new_up, new_moment_up, new_second_up = adam_update(factor_up, up_gradient, moment_up, second_up)

    keep, send = call(
        back_body,
        (info, slots, low, *downs),
        [shape_of((2 * toks, half), jnp.bfloat16)] * 2,
        2 * 2 * toks * 512 * width,
        scratch=[
            pltpu.VMEM((2 * toks, 512), jnp.bfloat16),
            pltpu.VMEM((NZ, 2 * toks, 256), jnp.bfloat16),
        ],
    )
    o0, o1 = call(
        finish_body,
        (info, dv, w4, b01, b2, b3, keep, swap_cores(send)),
        [shape_of((toks, half), jnp.bfloat16)] * 2,
        2 * 2 * toks * 128 * 1024,
        scratch=[pltpu.VMEM((2 * toks, 128), jnp.float32)],
    )
    layer_input_gradient = call(
        place_body, (info, o0, swap_cores(o1)), [shape_of((toks, width), jnp.bfloat16)], 0
    )[0]
    return (
        layer_input_gradient,
        new_down,
        new_up,
        new_moment_down,
        new_second_down,
        new_moment_up,
        new_second_up,
    )


def solution(mesh):
    in_specs = (
        P("fsdp", "tensor"),
        P("fsdp", "tensor"),
        P("fsdp", "tensor"),
        P("fsdp", "tensor"),
        P("fsdp"),
        P("fsdp"),
        P(),
        P("fsdp", None, "tensor"),
        P("fsdp", None, "tensor"),
        P("fsdp", None, "tensor"),
        P("fsdp", None, "tensor"),
        P("fsdp", None, "tensor"),
        P("fsdp", None, "tensor"),
    )
    out_specs = (
        P("fsdp", "tensor"),
        P("fsdp", None, "tensor"),
        P("fsdp", None, "tensor"),
        P("fsdp", None, "tensor"),
        P("fsdp", None, "tensor"),
        P("fsdp", None, "tensor"),
        P("fsdp", None, "tensor"),
    )

    return jax.shard_map(shards, mesh=mesh, in_specs=in_specs, out_specs=out_specs, check_vma=False)
```

```python
import math

import jax
import jax.numpy as jnp
from jax import lax
from jax.experimental import pallas as pl
from jax.experimental.pallas import tpu as pltpu
from jax.sharding import PartitionSpec as P

MODEL_WIDTH = 8192
ADAPTER_RANK = 16
NY, NZ, NC, NX = 4, 8, 2, 4


nf4_levels = (
    -1.0,
    -0.6962,
    -0.5251,
    -0.3949,
    -0.2844,
    -0.1848,
    -0.0911,
    0.0,
    0.0796,
    0.1609,
    0.2461,
    0.3379,
    0.4407,
    0.5626,
    0.723,
    1.0,
)
adapter_scale = 2.0
beta_one = 0.9
beta_two = 0.999
adam_step = 10.0
learn_rate = 0.05
decay_rate = 0.01
adam_eps = 1e-08
inverse_width = 1.0 / math.sqrt(MODEL_WIDTH)
coefficient = adapter_scale / math.sqrt(ADAPTER_RANK)


def flat_index(y, z, c, x):
    return ((y * NZ + z) * NC + c) * NX + x


def routed(value, route):
    pairs = []
    for y in range(NY):
        for z in range(NZ):
            for c in range(NC):
                for x in range(NX):
                    pairs.append((flat_index(y, z, c, x), flat_index(*route(y, z, c, x))))
    return lax.ppermute(value, ("fsdp", "tensor"), pairs)


def swap_cores(value):
    return routed(value, lambda y, z, c, x: (y, z, 1 - c, x))


def both_ways_z(value, k):
    return routed(value, lambda y, z, c, x: (y, (z + (k if c == 0 else -k)) % NZ, c, x))


def along_y(value, k):
    return routed(value, lambda y, z, c, x: ((y + k) % NY, z, c, x))


def along_x(value, k):
    return routed(value, lambda y, z, c, x: (y, z, c, (x + k) % NX))


def to_width_plane(value):
    return routed(value, lambda y, z, c, x: (x, z, c, y))


def adam_update(param, grad, moment, second):
    new_moment = beta_one * moment + (1.0 - beta_one) * grad
    new_second = beta_two * second + (1.0 - beta_two) * grad * grad
    corrected = new_moment / (1.0 - beta_one**adam_step)
    divisor = jnp.sqrt(new_second / (1.0 - beta_two**adam_step)) + adam_eps
    new_param = param - learn_rate * (corrected / divisor + decay_rate * param)
    return (new_param, new_moment, new_second)


def dequantize(quant_codes, block_scales):
    levels_out = jnp.zeros(quant_codes.shape, jnp.float32)
    for position in range(16):
        levels_out = jnp.where(quant_codes == position, nf4_levels[position], levels_out)
    row_count, col_count = quant_codes.shape
    blocks = block_scales.shape[1]
    scaled = levels_out.reshape(row_count, blocks, col_count // blocks) * block_scales[:, :, None]
    return scaled.reshape(row_count, col_count).astype(jnp.bfloat16)


def dot_nt(a, b):
    return lax.dot_general(a, b, (((1,), (1,)), ((), ())), preferred_element_type=jnp.float32)


def dot_nn(a, b):
    return lax.dot_general(a, b, (((1,), (0,)), ((), ())), preferred_element_type=jnp.float32)


PIECES = ((0, None), (1, 0), (1, 1), (2, 0), (2, 1), (3, 0), (3, 1), (4, None))


def chip_at(info, core, step):
    z = info[1]
    return jnp.where(core == 0, z - step, z + step) & 7


def block_of(info, core, piece):
    step, a = PIECES[piece]
    return chip_at(info, core, step) * 2 + (core if a is None else a)


def spread_rows(info, slots, low, jy):
    y, c = info[0], info[2]
    rows = []
    for piece in range(8):
        hit = slots == ((y - jy) & 3) * 16 + block_of(info, c, piece)
        rows.append(jnp.where(hit, low, jnp.zeros_like(low)))
    return jnp.concatenate(rows, axis=0)


def pick_rows(info, slots, scores):
    y, c = info[0], info[2]
    total = jnp.zeros((16, slots.shape[1]), jnp.float32)
    for jy in range(NY):
        for piece in range(8):
            hit = slots == ((y - jy) & 3) * 16 + block_of(info, c, piece)
            at = jy * 128 + piece * 16
            total = total + jnp.where(hit, scores[at : at + 16, :], 0.0)
    return total


def up_scores_body(info, slots_ref, d0, d1, b0, b1, b2, b3, out, turned, acc):
    toks = d0.shape[0]
    for h, dr in enumerate((d0, d1)):
        cols = slice(h * toks, (h + 1) * toks)
        acc[...] = dot_nt(jnp.concatenate([b[:128, :] for b in (b0, b1, b2, b3)], axis=0), dr[...])
        total = pick_rows(info, slots_ref[:, cols], acc) * coefficient
        out[:, cols] = total
        turned[:, (1 - h) * toks : (2 - h) * toks] = total


def scores_body(info, slots_ref, x0, x1, a0, a1, a2, a3, out, turned, acc):
    toks = x0.shape[0]
    for h, xr in enumerate((x0, x1)):
        cols = slice(h * toks, (h + 1) * toks)
        acc[...] = jnp.zeros_like(acc)

        @pl.loop(0, 2)
        def _(k, xr=xr):
            at = pl.ds(pl.multiple_of(k * 1024, 1024), 1024)
            acc[...] += dot_nt(jnp.concatenate([a[:, at] for a in (a0, a1, a2, a3)], axis=0), xr[:, at])

        total = pick_rows(info, slots_ref[:, cols], acc) * inverse_width
        out[:, cols] = total
        turned[:, (1 - h) * toks : (2 - h) * toks] = total


def spread_all(info, slots_ref, low_ref, toks, spread):
    for h in range(2):
        cols = slice(h * toks, (h + 1) * toks)
        low = low_ref[:, cols].astype(jnp.float32)
        for jy in range(NY):
            rows = spread_rows(info, slots_ref[:, cols], low, jy)
            spread[h, jy * 128 : (jy + 1) * 128, :] = rows.astype(jnp.bfloat16)


def down_terms_body(info, slots_ref, low_ref, x0, x1, o0, o1, o2, o3, spread):
    toks, width = x0.shape
    spread_all(info, slots_ref, low_ref, toks, spread)

    @pl.loop(0, width // 256)
    def _(k):
        at = pl.ds(pl.multiple_of(k * 256, 256), 256)
        down = dot_nn(spread[0], x0[:, at]) + dot_nn(spread[1], x1[:, at])
        down = (down * inverse_width).astype(jnp.bfloat16)
        for jy, out in enumerate((o0, o1, o2, o3)):
            out[:, at] = down[jy * 128 : (jy + 1) * 128]


def up_terms_body(info, slots_ref, low_ref, d0, d1, o0, o1, o2, o3, spread):
    spread_all(info, slots_ref, low_ref, d0.shape[0], spread)
    up = dot_nn(spread[0], d0[...]) + dot_nn(spread[1], d1[...])
    up = (up * coefficient).astype(jnp.bfloat16)
    for jy, out in enumerate((o0, o1, o2, o3)):
        out[...] = up[jy * 128 : (jy + 1) * 128]


def y_sums_body(r0, r1, r2, r3, u0, u1, u2, u3, *outs):
    width = r0.shape[1]
    at = 0
    for out in outs:
        rows = slice(at, at + out.shape[0])
        total = r0[rows, :].astype(jnp.float32) + r1[rows, :].astype(jnp.float32)
        total = total + r2[rows, :].astype(jnp.float32) + r3[rows, :].astype(jnp.float32)
        out[:, :width] = total.astype(out.dtype)
        total = u0[rows, :].astype(jnp.float32) + u1[rows, :].astype(jnp.float32)
        total = total + u2[rows, :].astype(jnp.float32) + u3[rows, :].astype(jnp.float32)
        out[:, width:] = total.astype(out.dtype)
        at += out.shape[0]


def z_sums_body(info, p0, r1, r2, r3, r4, own, other):
    c = info[2]
    mine = pl.ds(pl.multiple_of(c * 16, 16), 16)
    theirs = pl.ds(pl.multiple_of((1 - c) * 16, 16), 16)
    total = p0[...] + r4[...].astype(jnp.float32)
    for r in (r1, r2, r3):
        total = total + r[mine, :].astype(jnp.float32)
    own[...] = total
    total = r1[theirs, :].astype(jnp.float32) + r2[theirs, :].astype(jnp.float32)
    other[...] = total + r3[theirs, :].astype(jnp.float32)


def back_body(info, slots_ref, low_ref, a0, a1, a2, a3, keep, send, spread, by_step):
    toks = slots_ref.shape[1] // 2
    c = info[2]
    for h in range(2):
        cols = slice(h * toks, (h + 1) * toks)
        slots = slots_ref[:, cols]
        low = low_ref[:, cols].astype(jnp.float32)
        for jy in range(NY):
            turned = spread_rows(info, slots, low, jy).T
            spread[cols, jy * 128 : (jy + 1) * 128] = turned.astype(jnp.bfloat16)

    @pl.loop(0, NZ)
    def _(step):
        at = pl.ds(pl.multiple_of(chip_at(info, c, step) * 256, 256), 256)
        part = jnp.concatenate([a[:, at] for a in (a0, a1, a2, a3)], axis=0)
        by_step[step] = (dot_nn(spread[...], part) * inverse_width).astype(jnp.bfloat16)

    for piece, (step, a) in enumerate(PIECES):
        to = slice(piece * 128, (piece + 1) * 128)
        if a is None:
            first, second = by_step[step, :, :128], by_step[step, :, 128:]
            keep[:, to] = jnp.where(c == 0, first, second)
            send[:, to] = jnp.where(c == 0, second, first)
        else:
            keep[:, to] = by_step[step, :, a * 128 : (a + 1) * 128]
            send[:, to] = by_step[8 - step, :, a * 128 : (a + 1) * 128]


def base_body(info, dv, *refs):
    y, x = info[0], info[3]
    *weights, out = refs
    out[...] = jnp.zeros_like(out)

    @pl.loop(0, NY)
    def _(q):
        grads = dv[(x - y + q) & 3]
        at = 0
        for w in weights:
            rows = w[q] if len(w.shape) == 3 else jnp.concatenate([w[0, q], w[1, q]], axis=0)
            out[:, at : at + rows.shape[0]] += dot_nt(grads, rows)
            at += rows.shape[0]


def finish_body(info, dv, w4, b01, b2, b3, keep, came, o0, o1, acc):
    toks = o0.shape[0]
    base_body(info, dv, w4, acc)
    for h, out in enumerate((o0, o1)):
        rows = slice(h * toks, (h + 1) * toks)
        turned = slice((1 - h) * toks, (2 - h) * toks)
        at = 0
        for base in (b01, b2, b3, acc):
            cols = slice(at, at + base.shape[1])
            total = base[rows, :] + keep[rows, cols].astype(jnp.float32)
            total = total + came[turned, cols].astype(jnp.float32)
            out[:, cols] = total.astype(jnp.bfloat16)
            at += base.shape[1]


def place_body(info, own, other, out):
    c = info[2]
    for core, ref in ((c, own), (1 - c, other)):
        for piece in range(8):
            at = pl.multiple_of(block_of(info, core, piece) * 128, 128)
            out[:, pl.ds(at, 128)] = ref[:, piece * 128 : (piece + 1) * 128]


SCALARS = pl.BlockSpec(memory_space=pltpu.SMEM)
LOCAL = pl.BlockSpec(memory_space=pltpu.VMEM)


def shape_of(shape, dtype):
    return jax.ShapeDtypeStruct(shape, dtype)


def call(body, operands, outs, flops, scalars=True, scratch=()):
    vmem_count = len(operands) - (1 if scalars else 0)
    moved = sum(o.size * o.dtype.itemsize for o in operands)
    moved += sum(math.prod(o.shape) * jnp.dtype(o.dtype).itemsize for o in outs)
    return pl.pallas_call(
        body,
        out_shape=outs,
        in_specs=([SCALARS] if scalars else []) + [LOCAL] * vmem_count,
        out_specs=[LOCAL] * len(outs),
        scratch_shapes=list(scratch),
        compiler_params=pltpu.CompilerParams(vmem_limit_bytes=24 * 1024 * 1024),
        cost_estimate=pl.CostEstimate(flops=flops, bytes_accessed=moved, transcendentals=0),
    )(*operands)


def shards(
    layer_input,
    value_grad,
    quant_codes,
    block_scales,
    tenant_ids,
    live_counts,
    tenant_owner,
    factor_down,
    factor_up,
    moment_down,
    second_down,
    moment_up,
    second_up,
):
    toks, width = layer_input.shape
    values = value_grad.shape[1]
    wide = width + values
    half = width // 2
    seqs = tenant_ids.shape[0]
    seq_len = toks // seqs
    place = lax.axis_index("fsdp") * NX + lax.axis_index("tensor")
    info = (place // jnp.array([64, 8, 4, 1], jnp.int32)) % jnp.array([4, 8, 2, 4], jnp.int32)
    first = (place // 4) % 2 == 0

    def in_order(own, other, axis=0):
        low = jnp.where(first, own, other)
        high = jnp.where(first, other, own)
        return jnp.concatenate([low, high], axis=axis)

    matches = tenant_ids[:, None] == jnp.arange(tenant_owner.shape[0], dtype=jnp.int32)[None, :]
    slot_own = jnp.sum(jnp.where(matches, tenant_owner[None, :], 0), axis=1)

    ab = jnp.concatenate([factor_down[0], factor_up[0]], axis=1).astype(jnp.bfloat16)
    riders = jnp.broadcast_to(slot_own.astype(jnp.bfloat16)[:, None], (seqs, 128))
    swapped = swap_cores(jnp.concatenate([ab, riders], axis=1))
    chip_ab = in_order(ab, swapped[:, :wide])
    slot_other = swapped[:, wide].astype(jnp.int32)
    steps = [both_ways_z(chip_ab, k) for k in range(1, 4)]
    steps = [ab] + steps + [both_ways_z(ab, 4)]
    az = jnp.concatenate([s[:, :width] for s in steps], axis=0)
    downs = [az] + [along_y(az, j) for j in range(1, NY)]

    slot_all = jnp.concatenate([slot_own, slot_other])
    slots = jnp.broadcast_to(slot_all[:, None], (2 * seqs, seq_len)).reshape(1, 2 * toks)
    live_tok = jnp.arange(toks, dtype=jnp.int32) // seq_len < live_counts[0]
    d0 = jnp.where(live_tok[:, None], value_grad, jnp.zeros_like(value_grad))
    d1 = swap_cores(d0)
    x0, x1 = layer_input, swap_cores(layer_input)

    weight = to_width_plane(dequantize(quant_codes, block_scales))
    rider = jnp.concatenate([s[:, width:] for s in steps] + [weight], axis=0)
    ups = [rider] + [along_y(rider, j) for j in range(1, NY)]
    w0 = jnp.stack([u[128:] for u in ups])
    w1 = both_ways_z(in_order(w0[None], swap_cores(w0)[None]), 1)
    w2 = both_ways_z(w1, 1)
    w3 = both_ways_z(w2, 1)
    w4 = both_ways_z(jnp.where(first, w3[0], w3[1]), 1)
    chip_grad = jnp.concatenate([d0, d1], axis=0)
    dv = jnp.stack([chip_grad] + [along_x(chip_grad, j) for j in range(1, NX)])

    def base(*weights):
        columns = sum(w.size // 1024 for w in weights)
        return call(
            base_body,
            (info, dv, *weights),
            [shape_of((2 * toks, columns), jnp.float32)],
            2 * 2 * toks * columns * 1024,
        )[0]

    b01, b2, b3 = base(w0, w1), base(w2), base(w3)

    def rank_sums(body, operands, flops):
        own, turned = call(
            body,
            operands,
            [shape_of((ADAPTER_RANK, 2 * toks), jnp.float32)] * 2,
            flops,
            scratch=[pltpu.VMEM((512, toks), jnp.float32)],
        )
        pair = own + swap_cores(turned)
        total = pair
        for j in range(1, NX):
            total = total + along_x(pair, j)
        return total.astype(jnp.bfloat16)

    spread = pltpu.VMEM((2, 512, toks), jnp.bfloat16)
    rank_flops = 2 * 2 * toks * 512

    def row_terms(body, operands, columns):
        return call(
            body,
            operands,
            [shape_of((128, columns), jnp.bfloat16)] * NY,
            rank_flops * columns,
            scratch=[spread],
        )

    low = rank_sums(up_scores_body, (info, slots, d0, d1, *ups), rank_flops * values)
    terms = row_terms(down_terms_body, (info, slots, low, x0, x1), width)
    arrived = [terms[0]] + [along_y(terms[j], -j) for j in range(1, NY)]

    in_low = rank_sums(scores_body, (info, slots, x0, x1, *downs), rank_flops * width)
    terms = row_terms(up_terms_body, (info, slots, in_low, d0, d1), values)
    arrived += [terms[0]] + [along_y(terms[j], -j) for j in range(1, NY)]
    pieces = call(
        y_sums_body,
        tuple(arrived),
        [shape_of((16, wide), jnp.float32)]
        + [shape_of((32, wide), jnp.bfloat16)] * 3
        + [shape_of((16, wide), jnp.bfloat16)],
        4 * 128 * wide,
        scalars=False,
    )
    came = [both_ways_z(pieces[k], -k) for k in range(1, 5)]
    own, other = call(
        z_sums_body,
        (info, pieces[0], *came),
        [shape_of((16, wide), jnp.float32)] * 2,
        8 * 16 * wide,
    )
    gradient = own + swap_cores(other)
    down_gradient, up_gradient = gradient[None, :, :width], gradient[None, :, width:]
    new_down, new_moment_down, new_second_down = adam_update(
        factor_down, down_gradient, moment_down, second_down
    )
    new_up, new_moment_up, new_second_up = adam_update(factor_up, up_gradient, moment_up, second_up)

    keep, send = call(
        back_body,
        (info, slots, low, *downs),
        [shape_of((2 * toks, half), jnp.bfloat16)] * 2,
        2 * 2 * toks * 512 * width,
        scratch=[
            pltpu.VMEM((2 * toks, 512), jnp.bfloat16),
            pltpu.VMEM((NZ, 2 * toks, 256), jnp.bfloat16),
        ],
    )
    o0, o1 = call(
        finish_body,
        (info, dv, w4, b01, b2, b3, keep, swap_cores(send)),
        [shape_of((toks, half), jnp.bfloat16)] * 2,
        2 * 2 * toks * 128 * 1024,
        scratch=[pltpu.VMEM((2 * toks, 128), jnp.float32)],
    )
    layer_input_gradient = call(
        place_body, (info, o0, swap_cores(o1)), [shape_of((toks, width), jnp.bfloat16)], 0
    )[0]
    return (
        layer_input_gradient,
        new_down,
        new_up,
        new_moment_down,
        new_second_down,
        new_moment_up,
        new_second_up,
    )


def solution(mesh):
    in_specs = (
        P("fsdp", "tensor"),
        P("fsdp", "tensor"),
        P("fsdp", "tensor"),
        P("fsdp", "tensor"),
        P("fsdp"),
        P("fsdp"),
        P(),
        P("fsdp", None, "tensor"),
        P("fsdp", None, "tensor"),
        P("fsdp", None, "tensor"),
        P("fsdp", None, "tensor"),
        P("fsdp", None, "tensor"),
        P("fsdp", None, "tensor"),
    )
    out_specs = (
        P("fsdp", "tensor"),
        P("fsdp", None, "tensor"),
        P("fsdp", None, "tensor"),
        P("fsdp", None, "tensor"),
        P("fsdp", None, "tensor"),
        P("fsdp", None, "tensor"),
        P("fsdp", None, "tensor"),
    )

    return jax.shard_map(shards, mesh=mesh, in_specs=in_specs, out_specs=out_specs, check_vma=False)
```
